32 devices in a mesh: section: 2 (over core), expert: 8 (over z, x), dp: 2 (over y).
Axes of the slice: x: 2, y: 2, z: 4, core: 2. Of those that a mesh axis runs over, the one named last changes fastest.
Arguments:
- tokens: bfloat16 [2, 16, 65, 768], P(None, ('expert', 'dp')), may hold values from -6 to 6
- cotangent: bfloat16 [2, 16, 65, 768], P(None, ('expert', 'dp')), may hold values from -6 to 6
- routes: int32 [2, 2, 16, 65, 2], P('section', None, ('expert', 'dp')), may hold values from 0 to 7, all different within a row; in each aligned block of 65 rows (0 to 64, 65 to 129, ..., all dimensions but the last counted through in order) at most 25 rows name the same one
- norm1_gain: bfloat16 [2, 768], P('section', 'dp'), may hold values from 0.099609375 to 1.8984375
- qkv_weight: bfloat16 [2, 768, 2304], P('section', 'dp'), may hold values from -1 to 1
- out_weight: bfloat16 [2, 768, 768], P('section', 'dp'), may hold values from -1.25 to 1.25
- norm2_gain: bfloat16 [2, 768], P('section', 'dp'), may hold values from 0.099609375 to 1.8984375
- router_weight: bfloat16 [2, 768, 8], P('section', 'dp'), may hold values from -1 to 1
- expert_in: bfloat16 [2, 8, 768, 3072], P('section', 'expert', None, 'dp'), may hold values from -0.21875 to 0.21875
- expert_out: bfloat16 [2, 8, 3072, 768], P('section', 'expert', 'dp'), may hold values from -0.875 to 0.875
Outputs:
- boundary: float32 [2, 2, 16, 65, 768], P('section', None, ('expert', 'dp'))
- grad_norm1: float32 [2, 768], P('section', 'dp')
- grad_qkv: float32 [2, 768, 2304], P('section', 'dp')
- grad_proj: float32 [2, 768, 768], P('section', 'dp')
- grad_norm2: float32 [2, 768], P('section', 'dp')
- grad_router: float32 [2, 768, 8], P('section', 'dp')
- grad_expert_in: float32 [2, 8, 768, 3072], P('section', 'expert', None, 'dp')
- grad_expert_out: float32 [2, 8, 3072, 768], P('section', 'expert', 'dp')
The draws below stay inside these ranges and needn't reach their ends.
Inputs may be any that keep to these rules, and one draw needn't show every extreme that they name: `routes`: in every aligned block of 65 rows (the images of one device in one micro-batch of one section) no expert is named by more than 25 rows, a bound that some block reaches; the two experts of a token differ.
All inputs are finite; a program needn't handle non-finite values.
Results may differ from the reference program's by a relative error of at most 0.03.
Values may be sent and summed in bfloat16 or wider, within the bound.
No kernel may reach another device: no remote copies, remote signals or barrier semaphores. Data moves between devices by JAX's collectives and lax.ppermute only.
A program may use at most 192 MiB of HBM per device.

```python
import math
import jax
import jax.numpy as jnp
import numpy as np
from jax import lax

D = 768
HEADS = 12
HEAD = 64
FF = 3072
EXPERTS = 8
SEQ = 65
IMG_MB = 1
MB = 2
IMAGES = 16
CAP = 25
N_SECTION = 2


def draw_tokens(key, part):
    full_shape = (MB, IMAGES, SEQ, D)
    values = jnp.clip(jax.random.normal(key, full_shape, jnp.float32), -6.0, 6.0)
    return values.astype(jnp.bfloat16)


def draw_qkv_weight(key, part):
    weight_scale = D ** (-0.5)
    full_shape = (N_SECTION, D, 3 * D)
    values = jnp.clip(jax.random.normal(key, full_shape, jnp.float32), -6.0, 6.0) * weight_scale
    return values.astype(jnp.bfloat16)


def draw_router_weight(key, part):
    weight_scale = D ** (-0.5)
    full_shape = (N_SECTION, D, EXPERTS)
    values = jnp.clip(jax.random.normal(key, full_shape, jnp.float32), -6.0, 6.0) * weight_scale
    return values.astype(jnp.bfloat16)


def block_scale(key, dims, cuts, smallest, largest):
    loudness, own = 1.0, jax.random.fold_in(key, 6)
    for dim, blocks in cuts:
        draws = jnp.exp(jax.random.uniform(jax.random.fold_in(own, dim), (blocks,), jnp.float32, smallest / len(cuts), largest / len(cuts)))
        loudness = loudness * jnp.repeat(draws, dims[dim] // blocks).reshape([-1 if axis == dim else 1 for axis in range(len(dims))])
    return loudness


def shared_out(key, own, number, rows, count, top, bound, skew):
    sequence = jax.random.permutation(key, count)
    packed, usual = load_shares(count, rows * top, bound, skew, True), load_shares(count, rows * top, bound, skew, False)
    places = jnp.arange(count)

    def named(lengths, turn):
        used = int((lengths > 0).sum())
        fixed = max(1, used // 4)
        moved = fixed + (places - fixed + turn * (used - fixed)) % max(1, count - fixed)
        return jnp.zeros((count,), jnp.int32).at[sequence[jnp.where(places < fixed, places, moved)]].set(jnp.asarray(lengths, jnp.int32))

    lengths = jnp.where(number % 4 == 0, named(packed, number // 4), named(usual, number - number // 4 - 1))
    mixed = jax.random.permutation(jax.random.fold_in(own, 3), count)
    source_of, receiver = mixed[0:count // 2 * 2:2], mixed[1:count // 2 * 2:2]
    room = jnp.minimum(lengths[source_of] - 1, bound - lengths[receiver]) // 2
    room = jnp.where((source_of == sequence[0]) | (receiver == sequence[0]) | (lengths[receiver] == 0), 0, jnp.maximum(room, 0))
    moved = jax.random.randint(jax.random.fold_in(own, 4), (count // 2,), 0, 1 << 20) % (room + 1)
    lengths = lengths.at[source_of].add(-moved).at[receiver].add(moved)
    labels = jnp.searchsorted(jnp.cumsum(lengths), jnp.arange(rows * top), side="right").astype(jnp.int32)
    listing = labels.reshape(top, rows).T
    listing = listing[jax.random.permutation(jax.random.fold_in(own, 1), rows)]
    turn = jax.random.randint(jax.random.fold_in(own, 2), (rows, 1), 0, top)
    return jnp.take_along_axis(listing, (jnp.arange(top)[None, :] + turn) % top, axis=1)


def load_shares(amount, total, reach, lean, full):
    portions = [(1 << 20) // math.isqrt(standing ** lean) + 1 for standing in range(1, amount + 1)]
    largest = reach if full else min(reach, max(-(-total // amount), total * portions[0] // sum(portions)))
    least = 1 if total - largest >= amount - 1 else 0
    counts, surplus = [largest] + [least] * (amount - 1), total - largest - least * (amount - 1)
    while surplus > 0:
        candidates = [i for i in range(1, amount) if counts[i] < largest] or [i for i in range(1, amount) if counts[i] < reach]
        mass, budget = sum([portions[i] for i in candidates]), surplus
        for i in candidates:
            addition = min(reach - counts[i], max(1, budget * portions[i] // mass), surplus)
            counts[i] = counts[i] + addition
            surplus = surplus - addition
    return np.array(counts)


def noise(stream_key, extent, spread, most, cuts=(), kind=jnp.bfloat16):
    array = jax.random.normal(stream_key, extent, jnp.float32) * spread
    if len(cuts) > 0:
        array = block_scale(stream_key, extent, cuts, -0.22, 0.18) * array
    return jnp.clip(array, min=-most, max=most).astype(kind)


def setup_inputs(seed: int = 0) -> dict:
    arg_keys = jax.random.split(jax.random.key(seed), 11)
    tokens = draw_tokens(jax.random.fold_in(arg_keys[10], 71), 0)
    cotangent = noise(arg_keys[1], (MB, IMAGES, SEQ, D), 1.0, 6.0, ((1, 16),))
    routes_keys = jax.random.split(jax.random.fold_in(arg_keys[2], 1), N_SECTION * MB * IMAGES * SEQ // (IMG_MB * SEQ))
    routes_turns = jax.random.permutation(jax.random.fold_in(arg_keys[2], 3), N_SECTION * MB * IMAGES * SEQ // (IMG_MB * SEQ))
    routes = jax.vmap(lambda own, number: shared_out(jax.random.fold_in(arg_keys[2], 2), own, number, IMG_MB * SEQ, EXPERTS, 2, CAP, 2))(routes_keys, routes_turns).reshape((N_SECTION, MB, IMAGES, SEQ, 2))
    norm1_gain = jnp.clip(1.0 + 0.18 * jax.random.normal(arg_keys[3], (N_SECTION, D), jnp.float32), 0.099609375, 1.8984375).astype(jnp.bfloat16)
    qkv_weight = draw_qkv_weight(jax.random.fold_in(arg_keys[10], 71), 0)
    out_weight = noise(arg_keys[5], (N_SECTION, D, D), (D // 32) ** -0.5, 1.25, ((0, 2), (1, 2)))
    norm2_gain = jnp.clip(1.0 + 0.18 * jax.random.normal(arg_keys[6], (N_SECTION, D), jnp.float32), 0.099609375, 1.8984375).astype(jnp.bfloat16)
    router_weight = draw_router_weight(jax.random.fold_in(arg_keys[10], 71), 0)
    expert_in = noise(arg_keys[8], (N_SECTION, EXPERTS, D, FF), D ** -0.5, 0.21875, ((0, 2), (1, 8), (3, 2)))
    expert_out = noise(arg_keys[9], (N_SECTION, EXPERTS, FF, D), (FF // 64) ** -0.5, 0.875, ((0, 2), (1, 8), (2, 2)))
    return {"tokens": tokens, "cotangent": cotangent, "routes": routes, "norm1_gain": norm1_gain, "qkv_weight": qkv_weight, "out_weight": out_weight, "norm2_gain": norm2_gain, "router_weight": router_weight, "expert_in": expert_in, "expert_out": expert_out}


EPSILON = 1e-06

def norm_forward(values, norm_gain):
    center = values - lax.optimization_barrier(jnp.mean(values, axis=-1, keepdims=True))
    inverse = lax.rsqrt(lax.optimization_barrier(jnp.mean(center * center, axis=-1, keepdims=True)) + EPSILON)
    normed = center * inverse
    return (normed * norm_gain, normed, inverse)

def norm_backward(grad_out, normed, inverse, norm_gain):
    grad_hat = grad_out * norm_gain
    grad_gain = lax.optimization_barrier(jnp.sum(grad_out * normed, axis=0))
    grad_in = inverse * (grad_hat - lax.optimization_barrier(jnp.mean(grad_hat, axis=-1, keepdims=True)) - normed * lax.optimization_barrier(jnp.mean(grad_hat * normed, axis=-1, keepdims=True)))
    return (grad_in, grad_gain)

def gelu_slope(pre_act):
    return 0.5 * (1.0 + lax.erf(pre_act * 0.7071067811865476)) + pre_act * jnp.exp(-0.5 * pre_act * pre_act) * 0.3989422804014327

def round_keep(values):
    return lax.optimization_barrier(values.astype(jnp.bfloat16)).astype(jnp.float32)

def attention_forward(a_norm, qkv_weight):
    images = a_norm.shape[0] // SEQ
    qkv_rows = jnp.dot(a_norm, qkv_weight, preferred_element_type=jnp.float32).astype(jnp.bfloat16)
    shaped = qkv_rows.reshape(images, SEQ, 3, HEADS, HEAD).astype(jnp.float32)
    scores = jnp.einsum('ishd,ithd->ihst', shaped[:, :, 0], shaped[:, :, 1]) * HEAD ** (-0.5)
    row_max = lax.optimization_barrier(jnp.max(scores, axis=-1, keepdims=True))
    log_total = row_max + jnp.log(lax.optimization_barrier(jnp.sum(jnp.exp(scores - row_max), axis=-1, keepdims=True)))
    attn_probs = round_keep(jnp.exp(scores - log_total))
    attended = jnp.einsum('ihst,ithd->ishd', attn_probs, shaped[:, :, 2])
    attended = attended.astype(jnp.bfloat16).reshape(images * SEQ, HEADS * HEAD)
    return (qkv_rows, log_total, attended)

def attention_backward(grad_attended, qkv_rows, log_total):
    images = qkv_rows.shape[0] // SEQ
    shaped = qkv_rows.reshape(images, SEQ, 3, HEADS, HEAD).astype(jnp.float32)
    query_part = shaped[:, :, 0]
    key_part = shaped[:, :, 1]
    value_part = shaped[:, :, 2]
    score_scale = HEAD ** (-0.5)
    scores = jnp.einsum('ishd,ithd->ihst', query_part, key_part) * score_scale
    attn_probs = jnp.exp(scores - log_total)
    probs_low = round_keep(attn_probs)
    grad_heads = grad_attended.reshape(images, SEQ, HEADS, HEAD).astype(jnp.float32)
    grad_value = jnp.einsum('ihst,ishd->ithd', probs_low, grad_heads)
    grad_probs = jnp.einsum('ishd,ithd->ihst', grad_heads, value_part)
    grad_scores = attn_probs * (grad_probs - lax.optimization_barrier(jnp.sum(attn_probs * grad_probs, axis=-1, keepdims=True))) * score_scale
    grad_scores = round_keep(grad_scores)
    grad_query = jnp.einsum('ihst,ithd->ishd', grad_scores, key_part)
    grad_key = jnp.einsum('ihst,ishd->ithd', grad_scores, query_part)
    stacked = jnp.stack([grad_query, grad_key, grad_value], axis=2)
    return stacked.astype(jnp.bfloat16).reshape(images * SEQ, 3 * HEADS * HEAD)

def global_slots(route_ids):
    blocks = route_ids.shape[0] // IMG_MB
    flat_routes = route_ids.reshape(blocks, IMG_MB * SEQ * 2).astype(jnp.int32)
    onehot = (flat_routes[:, :, None] == jnp.arange(EXPERTS, dtype=jnp.int32)[None, None, :]).astype(jnp.int32)
    running = jnp.cumsum(onehot, axis=1) - 1
    slot_pos = lax.optimization_barrier(jnp.sum(onehot * running, axis=-1)).astype(jnp.int32)
    block_ids = jnp.arange(blocks, dtype=jnp.int32)[:, None]
    slot_place = flat_routes * (blocks * CAP) + block_ids * CAP + slot_pos
    return (slot_place.reshape(-1).astype(jnp.int32), blocks)

def one_expert(pieces):
    slot_rows, weight_in, weight_out = pieces
    pre_act = jnp.dot(slot_rows, weight_in, preferred_element_type=jnp.float32)
    hidden = jax.nn.gelu(pre_act, approximate=False).astype(jnp.bfloat16)
    return jnp.dot(hidden, weight_out, preferred_element_type=jnp.float32).astype(jnp.bfloat16)

def one_expert_back(pieces):
    slot_rows, slot_grads, weight_in, weight_out = pieces
    pre_act = jnp.dot(slot_rows, weight_in, preferred_element_type=jnp.float32)
    hidden = jax.nn.gelu(pre_act, approximate=False).astype(jnp.bfloat16)
    grad_weight_out = jnp.dot(hidden.T, slot_grads, preferred_element_type=jnp.float32)
    grad_hidden = jnp.dot(slot_grads, weight_out.T, preferred_element_type=jnp.float32)
    grad_pre = (grad_hidden * gelu_slope(pre_act)).astype(jnp.bfloat16)
    grad_weight_in = jnp.dot(slot_rows.T, grad_pre, preferred_element_type=jnp.float32)
    grad_slots = jnp.dot(grad_pre, weight_in.T, preferred_element_type=jnp.float32)
    return (grad_slots, grad_weight_in, grad_weight_out)

def layer_forward(layer_in, route_ids, weights):
    norm_one, weight_qkv, weight_proj, norm_two, weight_router, expert_in, expert_out = weights
    token_rows = layer_in.reshape(-1, D).astype(jnp.float32)
    a_full, hat_one, inv_one = norm_forward(token_rows, norm_one.astype(jnp.float32))
    a_norm = a_full.astype(jnp.bfloat16)
    qkv_rows, log_total, attended = attention_forward(a_norm, weight_qkv)
    residual = token_rows + jnp.dot(attended, weight_proj, preferred_element_type=jnp.float32)
    b_full, hat_two, inv_two = norm_forward(residual, norm_two.astype(jnp.float32))
    b_norm = b_full.astype(jnp.bfloat16)
    logits = jnp.dot(b_norm, weight_router, preferred_element_type=jnp.float32)
    router = jax.nn.softmax(logits, axis=-1)
    pair_ids = route_ids.reshape(-1, 2).astype(jnp.int32)
    gate_vals = jnp.take_along_axis(router, pair_ids, axis=1)
    slot_place, blocks = global_slots(route_ids)
    buffers = jnp.zeros((EXPERTS * blocks * CAP, D), jnp.bfloat16)
    buffers = buffers.at[slot_place].set(jnp.repeat(b_norm, 2, axis=0)).reshape(EXPERTS, blocks * CAP, D)
    slot_out = lax.map(one_expert, (buffers, expert_in, expert_out)).reshape(-1, D)
    expert_rows = slot_out[slot_place].reshape(-1, 2, D)
    layer_out = residual + lax.optimization_barrier(jnp.sum(gate_vals[:, :, None] * expert_rows.astype(jnp.float32), axis=1))
    kept_state = (a_norm, hat_one, inv_one, qkv_rows, log_total, attended, hat_two, inv_two, b_norm, router, pair_ids, gate_vals, slot_place, buffers, expert_rows)
    return (layer_out, kept_state)

def layer_backward(grad_in, kept_state, weights):
    norm_one, weight_qkv, weight_proj, norm_two, weight_router, expert_in, expert_out = weights
    a_norm, hat_one, inv_one, qkv_rows, log_total, attended, hat_two, inv_two, b_norm, router, pair_ids, gate_vals, slot_place, buffers, expert_rows = kept_state
    grad_gate = lax.optimization_barrier(jnp.sum(grad_in[:, None, :] * expert_rows.astype(jnp.float32), axis=-1))
    grad_rows = (gate_vals[:, :, None] * grad_in[:, None, :]).astype(jnp.bfloat16).reshape(-1, D)
    grad_buffers = jnp.zeros(buffers.reshape(-1, D).shape, jnp.bfloat16)
    grad_buffers = grad_buffers.at[slot_place].set(grad_rows).reshape(buffers.shape)
    grad_slots, grad_exp_in, grad_exp_out = lax.map(one_expert_back, (buffers, grad_buffers, expert_in, expert_out))
    grad_b_expert = lax.optimization_barrier(jnp.sum(grad_slots.reshape(-1, D)[slot_place].reshape(-1, 2, D), axis=1))
    choose = (pair_ids[:, :, None] == jnp.arange(EXPERTS, dtype=jnp.int32)[None, None, :]).astype(jnp.float32)
    grad_prob = lax.optimization_barrier(jnp.sum(choose * grad_gate[:, :, None], axis=1))
    grad_logit = router * (grad_prob - lax.optimization_barrier(jnp.sum(router * grad_prob, axis=-1, keepdims=True)))
    grad_logit = grad_logit.astype(jnp.bfloat16)
    grad_router_w = jnp.dot(b_norm.T, grad_logit, preferred_element_type=jnp.float32)
    grad_b = jnp.dot(grad_logit, weight_router.T, preferred_element_type=jnp.float32) + grad_b_expert
    grad_resid_norm, grad_gain_two = norm_backward(grad_b, hat_two, inv_two, norm_two.astype(jnp.float32))
    grad_resid = grad_in + grad_resid_norm
    grad_low = grad_resid.astype(jnp.bfloat16)
    grad_proj_w = jnp.dot(attended.T, grad_low, preferred_element_type=jnp.float32)
    grad_attended = jnp.dot(grad_low, weight_proj.T, preferred_element_type=jnp.float32).astype(jnp.bfloat16)
    grad_qkv_rows = attention_backward(grad_attended, qkv_rows, log_total)
    grad_qkv_w = jnp.dot(a_norm.T, grad_qkv_rows, preferred_element_type=jnp.float32)
    grad_a = jnp.dot(grad_qkv_rows, weight_qkv.T, preferred_element_type=jnp.float32)
    grad_token_norm, grad_gain_one = norm_backward(grad_a, hat_one, inv_one, norm_one.astype(jnp.float32))
    grad_tokens = grad_resid + grad_token_norm
    return (grad_tokens, (grad_gain_one, grad_qkv_w, grad_proj_w, grad_gain_two, grad_router_w, grad_exp_in, grad_exp_out))

def reference(tokens, cotangent, routes, norm1_gain, qkv_weight, out_weight, norm2_gain, router_weight, expert_in, expert_out):
    every_weight = (norm1_gain, qkv_weight, out_weight, norm2_gain, router_weight, expert_in, expert_out)
    first_weights = tuple((member[0] for member in every_weight))
    second_weights = tuple((member[1] for member in every_weight))
    first_sums = tuple((jnp.zeros(member.shape, jnp.float32) for member in first_weights))
    second_sums = tuple((jnp.zeros(member.shape, jnp.float32) for member in second_weights))
    grad_inputs = []
    outputs = []
    for micro_index in range(MB):
        first_out, first_state = layer_forward(tokens[micro_index], routes[0, micro_index], first_weights)
        passed = first_out.astype(jnp.bfloat16).reshape(IMAGES, SEQ, D)
        second_out, second_state = layer_forward(passed, routes[1, micro_index], second_weights)
        start_grad = cotangent[micro_index].reshape(-1, D).astype(jnp.float32)
        second_grad, second_terms = layer_backward(start_grad, second_state, second_weights)
        first_grad, first_terms = layer_backward(round_keep(second_grad), first_state, first_weights)
        first_sums = tuple((first_term + second_term for first_term, second_term in zip(first_sums, first_terms)))
        second_sums = tuple((first_term + second_term for first_term, second_term in zip(second_sums, second_terms)))
        grad_inputs.append(first_grad.reshape(IMAGES, SEQ, D))
        outputs.append(second_out.reshape(IMAGES, SEQ, D))
    boundary = jnp.stack([jnp.stack(grad_inputs), jnp.stack(outputs)])
    stacked = [jnp.stack([first_term, second_term]) for first_term, second_term in zip(first_sums, second_sums)]
    return (boundary, stacked[0], stacked[1], stacked[2], stacked[3], stacked[4], stacked[5], stacked[6])
```

```python
import functools

import jax
import jax.numpy as jnp
import numpy as np
from jax import lax
from jax.experimental import pallas as pl
from jax.experimental.pallas import tpu as pltpu
from jax.sharding import PartitionSpec as P

HEAD = 64
EPSILON = 1e-06
BF = jnp.bfloat16
F32 = jnp.float32
SCALE = HEAD ** (-0.5)


def dot(a, b):
    return jnp.dot(a, b, preferred_element_type=F32)


def dot_nt(a, b):
    return lax.dot_general(a, b, (((1,), (1,)), ((), ())), preferred_element_type=F32)


def dot_tn(a, b):
    return lax.dot_general(a, b, (((0,), (0,)), ((), ())), preferred_element_type=F32)


def row_mean(v):
    return jnp.mean(v, axis=-1, keepdims=True)


def norm_parts(values):
    center = values - row_mean(values)
    inverse = lax.rsqrt(row_mean(center * center) + EPSILON)
    return center * inverse, inverse


def norm_backward(grad_out, normed, inverse, gain):
    grad_hat = grad_out * gain
    return inverse * (grad_hat - row_mean(grad_hat) - normed * row_mean(grad_hat * normed))


def softmax_router(b_norm, router_rows):
    logits = dot_nt(b_norm, router_rows)
    e = jnp.exp(logits - jnp.max(logits, axis=-1, keepdims=True))
    return e / jnp.sum(e, axis=-1, keepdims=True)


def expert_choice(routes_col, j, experts):
    rows = routes_col.shape[0]
    ids = lax.broadcasted_iota(jnp.int32, (rows, experts), 1)
    return (routes_col[:, j : j + 1] == ids).astype(F32)


def slots_by_token(routes_col, sid_row):
    rows = routes_col.shape[0]
    want, place = sid_row[0:1, :], sid_row[1:2, :].astype(F32)
    m0 = (routes_col[:, 0:1] == want).astype(F32)
    m1 = (routes_col[:, 1:2] == want).astype(F32)
    r = lax.broadcasted_iota(jnp.int32, (rows, rows), 0)
    c = lax.broadcasted_iota(jnp.int32, (rows, rows), 1)
    before = (c < r).astype(F32).astype(BF)
    pos = dot(before, (m0 + m1).astype(BF))
    here = (pos == place).astype(F32)
    return (m0 * here).astype(BF), (m1 * here).astype(BF)


def slots_by_slot(routes_row, sid_col):
    rows = routes_row.shape[1]
    want, place = sid_col[:, 0:1], sid_col[:, 1:2].astype(F32)
    m0 = (routes_row[0:1, :] == want).astype(F32)
    m1 = (routes_row[1:2, :] == want).astype(F32)
    r = lax.broadcasted_iota(jnp.int32, (rows, rows), 0)
    c = lax.broadcasted_iota(jnp.int32, (rows, rows), 1)
    before = (r < c).astype(F32).astype(BF)
    pos = dot((m0 + m1).astype(BF), before)
    here = (pos == place).astype(F32)
    return (m0 * here).astype(BF), (m1 * here).astype(BF)


def pair_masks():
    lane = lax.broadcasted_iota(jnp.int32, (1, 2 * HEAD), 1)
    first = (lane < HEAD).astype(F32)
    return first.astype(BF), (1.0 - first).astype(BF), first


def pair_probs(q2, k2, ma, mb, tokens):
    qs = jnp.concatenate([q2 * ma, q2 * mb], axis=0)
    scores = dot_nt(qs, k2) * SCALE
    col = lax.broadcasted_iota(jnp.int32, scores.shape, 1)
    scores = jnp.where(col < tokens, scores, -1e30)
    e = jnp.exp(scores - jnp.max(scores, axis=-1, keepdims=True))
    return qs, e / jnp.sum(e, axis=-1, keepdims=True)


def weight_copies(sel, half, d, own, swapped, dst, sem, base):
    near = pl.multiple_of(d * half, half)
    far = pl.multiple_of((1 - d) * half, half)

    def copies(src):
        return (
            pltpu.make_async_copy(src[0], dst.at[pl.ds(near, half)], sem.at[base]),
            pltpu.make_async_copy(src[1], dst.at[pl.ds(far, half)], sem.at[base + 1]),
        )

    @pl.when(sel)
    def _():
        for copy in copies(own):
            copy.start()

    @pl.when(jnp.logical_not(sel))
    def _():
        for copy in copies(swapped):
            copy.start()

    def wait():
        for copy in copies(own):
            copy.wait()

    return wait


def forward_body(layer, tokens, experts, second, *refs):
    if second:
        (ids, ret_p, r_p, small_p, rc_p, cot, small, rc, rr, sid_row, sid_col) = refs[:11]
        refs = refs[11:]
    else:
        (ids, x_ref, small, rr, sid_col) = refs[:5]
        refs = refs[5:]
    weights, refs = refs[:8], refs[8:]
    if second:
        send, r_out, qkv_out, attn_out, a_out, x_out, wq, wp, sem = refs
    else:
        send, r_out, qkv_out, attn_out, a_out, wq, wp, sem = refs
    width = wq.shape[0]
    sel = ids[0] == layer
    d = ids[1]
    half = width // 2
    wait_q = weight_copies(sel, half, d, weights[0:2], weights[2:4], wq, sem, 0)
    wait_p = weight_copies(sel, half, d, weights[4:6], weights[6:8], wp, sem, 2)
    if second:
        rows, routes_p = r_p[...], rc_p[...]
        normed, _ = norm_parts(rows)
        b_prev = (normed * small_p[1:2, :].astype(F32)).astype(BF)
        router = softmax_router(b_prev, small_p[2:, :])
        d0, d1 = slots_by_token(routes_p, sid_row[...])
        total = rows
        for j, dj in ((0, d0), (1, d1)):
            gate = jnp.sum(router * expert_choice(routes_p, j, experts), axis=-1, keepdims=True)
            total = total + gate * dot(dj, ret_p[...]).astype(BF).astype(F32)
        x = total.astype(BF)
        x_out[...] = x
    else:
        x = x_ref[...]
    x = x.astype(F32)
    normed, _ = norm_parts(x)
    a_norm = (normed * small[0:1, :].astype(F32)).astype(BF)
    a_out[...] = a_norm
    wait_q()
    qkv_out[...] = dot(a_norm, wq[...]).astype(BF)
    ma, mb, first = pair_masks()
    rows = x.shape[0]
    for p in range(width // (2 * HEAD)):
        at = p * 2 * HEAD
        q2 = qkv_out[:, at : at + 2 * HEAD]
        k2 = qkv_out[:, width + at : width + at + 2 * HEAD]
        v2 = qkv_out[:, 2 * width + at : 2 * width + at + 2 * HEAD]
        _, probs = pair_probs(q2, k2, ma, mb, tokens)
        o = dot(probs.astype(BF), v2)
        attn_out[:, at : at + 2 * HEAD] = (o[:rows] * first + o[rows:] * (1.0 - first)).astype(BF)
    wait_p()
    r = x + dot(attn_out[...], wp[...])
    r_out[...] = r
    normed, _ = norm_parts(r)
    b_norm = (normed * small[1:2, :].astype(F32)).astype(BF)
    t0, t1 = slots_by_slot(rr[...], sid_col[...])
    send[:, 0:width] = dot(t0 + t1, b_norm).astype(BF)
    if second:
        router = softmax_router(b_norm, small[2:, :])
        routes = rc[...]
        send[:, width:] = scatter_grads(router, routes, cot[...].astype(F32), t0, t1, experts)


def scatter_grads(router, routes, grad, t0, t1, experts):
    total = None
    for j, tj in ((0, t0), (1, t1)):
        gate = jnp.sum(router * expert_choice(routes, j, experts), axis=-1, keepdims=True)
        part = dot(tj, (gate * grad).astype(BF))
        total = part if total is None else total + part
    return total.astype(BF)


def backward_body(layer, tokens, experts, last, *refs):
    if last:
        (ids, ret, dsl, grad, r_ref, x_ref, qkv, small, rc, sid_row) = refs[:10]
        refs = refs[10:]
    else:
        (ids, ret, grad, r_ref, x_ref, qkv, small, rc, sid_row) = refs[:9]
        (r_p, small_p, rc_p, rr_p, sid_col) = refs[9:14]
        refs = refs[14:]
    weights, refs = refs[:8], refs[8:]
    if last:
        dqkv_out, dr_out, sm_out, dh_out, wq, wp, sem = refs
    else:
        dqkv_out, dr_out, sm_out, out_ref, c_out, send, wq, wp, sem = refs
    width = wq.shape[0]
    sel = ids[0] == layer
    d = ids[1]
    half = width // 2
    wait_p = weight_copies(sel, half, d, weights[4:6], weights[6:8], wp, sem, 2)
    wait_q = weight_copies(sel, half, d, weights[0:2], weights[2:4], wq, sem, 0)
    c = grad[...].astype(F32)
    r = r_ref[...]
    hat2, inv2 = norm_parts(r)
    gain2 = small[1:2, :].astype(F32)
    b_norm = (hat2 * gain2).astype(BF)
    router = softmax_router(b_norm, small[2:, :])
    routes = rc[...]
    d0, d1 = slots_by_token(routes, sid_row[...])
    grad_prob = jnp.zeros(router.shape, F32)
    total = r
    for j, dj in ((0, d0), (1, d1)):
        choice = expert_choice(routes, j, experts)
        rows_j = dot(dj, ret[:, 0:width]).astype(BF).astype(F32)
        grad_prob = grad_prob + choice * jnp.sum(c * rows_j, axis=-1, keepdims=True)
        if not last:
            gate = jnp.sum(router * choice, axis=-1, keepdims=True)
            total = total + gate * rows_j
    if not last:
        out_ref[...] = total
    slot_grads = dsl[...] if last else ret[:, width:]
    grad_b = dot(d0 + d1, slot_grads)
    grad_logit = router * (grad_prob - jnp.sum(router * grad_prob, axis=-1, keepdims=True))
    grad_logit = grad_logit.astype(BF)
    sm_out[2:, :] = dot_tn(grad_logit, b_norm)
    grad_b = grad_b + dot(grad_logit, small[2:, :])
    sm_out[1:2, :] = jnp.sum(grad_b * hat2, axis=0, keepdims=True)
    grad_r = c + norm_backward(grad_b, hat2, inv2, gain2)
    grad_low = grad_r.astype(BF)
    dr_out[...] = grad_low
    wait_p()
    grad_attn = dot_nt(grad_low, wp[...]).astype(BF)
    ma, mb, first = pair_masks()
    rows = r.shape[0]
    for p in range(width // (2 * HEAD)):
        at = p * 2 * HEAD
        q2 = qkv[:, at : at + 2 * HEAD]
        k2 = qkv[:, width + at : width + at + 2 * HEAD]
        v2 = qkv[:, 2 * width + at : 2 * width + at + 2 * HEAD]
        g2 = grad_attn[:, at : at + 2 * HEAD]
        qs, probs = pair_probs(q2, k2, ma, mb, tokens)
        gs = jnp.concatenate([g2 * ma, g2 * mb], axis=0)
        grad_v = dot_tn(probs.astype(BF), gs)
        grad_p = dot_nt(gs, v2)
        grad_s = probs * (grad_p - jnp.sum(probs * grad_p, axis=-1, keepdims=True)) * SCALE
        grad_s = grad_s.astype(BF)
        gq = dot(grad_s, k2)
        grad_k = dot_tn(grad_s, qs)
        dqkv_out[:, at : at + 2 * HEAD] = (gq[:rows] * first + gq[rows:] * (1.0 - first)).astype(BF)
        dqkv_out[:, width + at : width + at + 2 * HEAD] = grad_k.astype(BF)
        dqkv_out[:, 2 * width + at : 2 * width + at + 2 * HEAD] = grad_v.astype(BF)
    wait_q()
    grad_a = dot_nt(dqkv_out[...], wq[...])
    hat1, inv1 = norm_parts(x_ref[...].astype(F32))
    sm_out[0:1, :] = jnp.sum(grad_a * hat1, axis=0, keepdims=True)
    grad_h = grad_r + norm_backward(grad_a, hat1, inv1, small[0:1, :].astype(F32))
    if last:
        dh_out[...] = grad_h
    else:
        c_low = grad_h.astype(BF)
        c_out[...] = c_low
        normed, _ = norm_parts(r_p[...])
        b_prev = (normed * small_p[1:2, :].astype(F32)).astype(BF)
        router_p = softmax_router(b_prev, small_p[2:, :])
        t0, t1 = slots_by_slot(rr_p[...], sid_col[...])
        send[...] = scatter_grads(router_p, rc_p[...], c_low.astype(F32), t0, t1, experts)


def chosen_copies(sel, own, swapped, dst, sem):
    def start(src):
        for i, (a, b) in enumerate(zip(src, dst)):
            pltpu.make_async_copy(a, b, sem.at[i]).start()

    @pl.when(sel)
    def _():
        start(own)

    @pl.when(jnp.logical_not(sel))
    def _():
        start(swapped)

    return [functools.partial(lambda a, b, i: pltpu.make_async_copy(a, b, sem.at[i]).wait(), a, b, i) for i, (a, b) in enumerate(zip(own, dst))]


FCHUNK = 256


def gelu_parts(pre):
    half_erf = 0.5 * (1.0 + lax.erf(pre * 0.7071067811865476))
    slope = half_erf + pre * jnp.exp(-0.5 * pre * pre) * 0.3989422804014327
    return pre * half_erf, slope


def expert_forward_body(layer, ids, g, own_in, own_out, sw_in, sw_out, res, hid, slope, win, wout, sem):
    waits = chosen_copies(ids[0] == layer, (own_in, own_out), (sw_in, sw_out), (win, wout), sem)
    waits[0]()
    for f in range(0, win.shape[1], FCHUNK):
        pre = dot(g[...], win[:, f : f + FCHUNK])
        act, grad = gelu_parts(pre)
        hid[:, f : f + FCHUNK] = act.astype(BF)
        slope[:, f : f + FCHUNK] = grad.astype(BF)
    waits[1]()
    res[...] = dot(hid[...], wout[...]).astype(BF)


def expert_both_body(layer, ids, g, own_in, own_out, sw_in, sw_out, res, hid, dpre, win, wout, sem):
    waits = chosen_copies(ids[0] == layer, (own_in, own_out), (sw_in, sw_out), (win, wout), sem)
    width = win.shape[0]
    waits[0]()
    waits[1]()
    for f in range(0, win.shape[1], FCHUNK):
        pre = dot(g[:, :width], win[:, f : f + FCHUNK])
        back = dot_nt(g[:, width:], wout[f : f + FCHUNK, :])
        act, grad = gelu_parts(pre)
        hid[:, f : f + FCHUNK] = act.astype(BF)
        dpre[:, f : f + FCHUNK] = (back * grad).astype(BF)
    res[:, :width] = dot(hid[...], wout[...]).astype(BF)
    res[:, width:] = dot_nt(dpre[...], win[...]).astype(BF)


def expert_backward_body(layer, ids, g, slope, own_in, own_out, sw_in, sw_out, res, dpre, win, wout, sem):
    waits = chosen_copies(ids[0] == layer, (own_in, own_out), (sw_in, sw_out), (win, wout), sem)
    waits[1]()
    for f in range(0, win.shape[1], FCHUNK):
        back = dot_nt(g[...], wout[f : f + FCHUNK, :])
        dpre[:, f : f + FCHUNK] = (back * slope[:, f : f + FCHUNK].astype(F32)).astype(BF)
    waits[0]()
    res[...] = dot_nt(dpre[...], win[...]).astype(BF)


def expert_grads_body(ids, *refs):
    zero, one = refs[:8], refs[8:14]
    gin, gout, g_all, h_all, d_all, p_all, sem = refs[14:]
    rows = g_all.shape[0] // 2
    width = g_all.shape[1]

    def copies(layer):
        plan = []
        for i in range(2):
            part = pl.ds(i * rows, rows)
            if layer == 0:
                srcs = zero[4 * i : 4 * i + 4]
            else:
                gd, h, p = one[3 * i : 3 * i + 3]
                srcs = (gd.at[:, pl.ds(0, width)], h, gd.at[:, pl.ds(width, width)], p)
            for k, (src, dst) in enumerate(zip(srcs, (g_all, h_all, d_all, p_all))):
                plan.append(pltpu.make_async_copy(src, dst.at[part], sem.at[4 * i + k]))
        return plan

    @pl.when(ids[0] == 0)
    def _():
        for copy in copies(0):
            copy.start()

    @pl.when(ids[0] != 0)
    def _():
        for copy in copies(1):
            copy.start()

    for copy in copies(0):
        copy.wait()
    for f in range(0, h_all.shape[1], FCHUNK):
        gout[f : f + FCHUNK, :] = dot_tn(h_all[:, f : f + FCHUNK], d_all[...])
    for f in range(0, width, FCHUNK):
        gin[f : f + FCHUNK, :] = dot_tn(g_all[:, f : f + FCHUNK], p_all[...])


VM = pltpu.VMEM
SPECS = {
    "v": pl.BlockSpec(memory_space=pltpu.VMEM),
    "s": pl.BlockSpec(memory_space=pltpu.SMEM),
    "a": pl.BlockSpec(memory_space=pl.ANY),
}


def kernel_call(name, body, outs, ins, spaces, scratch):
    return pl.pallas_call(
        body,
        out_shape=[jax.ShapeDtypeStruct(shape, dtype) for shape, dtype in outs],
        in_specs=[SPECS[c] for c in spaces],
        out_specs=[SPECS["v"] for _ in outs],
        scratch_shapes=scratch,
        name=name,
    )(*ins)


def shards(
    tokens,
    cotangent,
    routes,
    norm1_gain,
    qkv_weight,
    out_weight,
    norm2_gain,
    router_weight,
    expert_in,
    expert_out,
):
    sec = lax.axis_index("section")
    dpi = lax.axis_index("dp")
    experts = router_weight.shape[2]
    pair = lax.axis_size("dp")
    group = lax.axis_size("expert")
    micro, images, seq, width = tokens.shape
    count = images * seq
    half = width // pair
    ff = expert_in.shape[3]
    rows = -(-count // 16) * 16
    capacity = max(2, (3 * count + experts - 1) // experts)
    capacity = -(-capacity // 8) * 8
    slots = experts * pair * capacity
    ids = jnp.stack([sec, dpi]).astype(jnp.int32)
    is0 = sec == 0
    swap = [(0, 1), (1, 0)]

    def across(v):
        return lax.ppermute(v, "section", swap)

    def to_section(v, target):
        return lax.ppermute(v, "section", [(1 - target, target)])

    def along(v):
        return lax.ppermute(v, "dp", swap)

    def along_in(v, section):
        pairs = [(section * pair, section * pair + 1), (section * pair + 1, section * pair)]
        return lax.ppermute(v, ("section", "dp"), pairs)

    wq, wp = qkv_weight[0], out_weight[0]
    win, wout = expert_in[0, 0], expert_out[0, 0]
    pack = jnp.concatenate([norm1_gain, norm2_gain, router_weight[0].T], axis=0)
    pack_far = along(pack)
    pack_full = jnp.concatenate(
        [jnp.where(dpi == 0, pack, pack_far), jnp.where(dpi == 0, pack_far, pack)], axis=1
    )
    pack_other = across(pack_full)
    small = (jnp.where(is0, pack_full, pack_other), jnp.where(is0, pack_other, pack_full))
    q_far0 = along_in(wq, 0)
    p_far0 = along_in(wp, 0)
    q_near, p_near = across(wq), across(wp)
    q_sf0, p_sf0 = to_section(q_far0, 1), to_section(p_far0, 1)
    held_q, held_p, q_far0, p_far0 = lax.optimization_barrier((wq, wp, q_far0, p_far0))
    q_far1 = along_in(held_q, 1)
    p_far1 = along_in(held_p, 1)
    q_sf1, p_sf1 = to_section(q_far1, 0), to_section(p_far1, 0)
    weights = (
        (wq, q_far0, q_near, q_sf0, wp, p_far0, p_near, p_sf0),
        (wq, q_far1, q_near, q_sf1, wp, p_far1, p_near, p_sf1),
    )
    win_sw, wout_sw = across(win), across(wout)

    mine = routes[0]
    own_route = jnp.where(is0, mine[0], mine[1])
    sent_route = jnp.where(is0, mine[1], mine[0])
    got_route = across(sent_route)
    fill = ((0, rows - count), (0, 0))

    def padded_route(r):
        return jnp.pad(r.reshape(count, 2), fill, constant_values=-1)

    rc = (
        padded_route(jnp.where(is0, own_route, got_route)),
        padded_route(jnp.where(is0, got_route, own_route)),
    )
    rr = (rc[0].T, rc[1].T)
    sid = np.arange(slots)
    sid_np = np.stack([sid // (pair * capacity), sid % capacity]).astype(np.int32)
    sid_row, sid_col = jnp.asarray(sid_np), jnp.asarray(sid_np.T.copy())

    def own_micro(v):
        return jnp.pad(jnp.where(is0, v[0], v[1]).reshape(count, width), fill)

    x0 = own_micro(tokens)
    cot = own_micro(cotangent)

    wscratch = [
        pltpu.VMEM((width, 3 * width), BF),
        pltpu.VMEM((width, width), BF),
        pltpu.SemaphoreType.DMA((4,)),
    ]
    escratch = [pltpu.VMEM((width, ff), BF), pltpu.VMEM((ff, width), BF), pltpu.SemaphoreType.DMA((2,))]

    def exchange(v):
        return lax.all_to_all(v, ("expert", "dp"), split_axis=0, concat_axis=0, tiled=True)

    token_outs = [((rows, width), F32), ((rows, 3 * width), BF), ((rows, width), BF), ((rows, width), BF)]
    send, r0, qkv0, attn0, a0 = kernel_call(
        "forward_first",
        functools.partial(forward_body, 0, count, experts, False),
        [((slots, width), BF)] + token_outs,
        (ids, x0, small[0], rr[0], sid_col) + weights[0],
        "svvvv" + "a" * 8,
        wscratch,
    )
    g0 = exchange(send)
    res0, hid0, slope0 = kernel_call(
        "experts_first",
        functools.partial(expert_forward_body, 0),
        [((slots, width), BF), ((slots, ff), BF), ((slots, ff), BF)],
        (ids, g0, win, wout, win_sw, wout_sw),
        "svaaaa",
        escratch,
    )
    ret0 = exchange(res0)
    send, r1, qkv1, attn1, a1, x1 = kernel_call(
        "forward_second",
        functools.partial(forward_body, 1, count, experts, True),
        [((slots, 2 * width), BF)] + token_outs + [((rows, width), BF)],
        (ids, ret0, r0, small[0], rc[0], cot, small[1], rc[1], rr[1], sid_row, sid_col) + weights[1],
        "s" + "v" * 10 + "a" * 8,
        wscratch,
    )
    gd1 = exchange(send)
    res1, hid1, dpre1 = kernel_call(
        "experts_second",
        functools.partial(expert_both_body, 1),
        [((slots, 2 * width), BF), ((slots, ff), BF), ((slots, ff), BF)],
        (ids, gd1, win, wout, win_sw, wout_sw),
        "svaaaa",
        escratch,
    )
    ret1 = exchange(res1)
    back_outs = [((rows, 3 * width), BF), ((rows, width), BF), ((experts + 2, width), F32)]
    dq1, dr1, sm1, out1, c0, send = kernel_call(
        "backward_second",
        functools.partial(backward_body, 1, count, experts, False),
        back_outs + [((rows, width), F32), ((rows, width), BF), ((slots, width), BF)],
        (ids, ret1, cot, r1, x1, qkv1, small[1], rc[1], sid_row, r0, small[0], rc[0], rr[0], sid_col)
        + weights[1],
        "s" + "v" * 13 + "a" * 8,
        wscratch,
    )
    d0 = exchange(send)
    res0b, dpre0 = kernel_call(
        "experts_last",
        functools.partial(expert_backward_body, 0),
        [((slots, width), BF), ((slots, ff), BF)],
        (ids, d0, slope0, win, wout, win_sw, wout_sw),
        "svvaaaa",
        escratch,
    )
    ret0b = exchange(res0b)
    dq0, dr0, sm0, dh0 = kernel_call(
        "backward_first",
        functools.partial(backward_body, 0, count, experts, True),
        back_outs + [((rows, width), F32)],
        (ids, ret0, ret0b, c0, r0, x0, qkv0, small[0], rc[0], sid_row) + weights[0],
        "s" + "v" * 9 + "a" * 8,
        wscratch,
    )

    o_g0, o_hid0, o_d0, o_dpre0 = (to_section(v, 0) for v in (g0, hid0, d0, dpre0))
    o_gd1, o_hid1, o_dpre1 = (to_section(v, 1) for v in (gd1, hid1, dpre1))
    gin, gout = kernel_call(
        "expert_grads",
        expert_grads_body,
        [((width, ff), F32), ((ff, width), F32)],
        (ids, g0, hid0, d0, dpre0, o_g0, o_hid0, o_d0, o_dpre0, gd1, hid1, dpre1, o_gd1, o_hid1, o_dpre1),
        "s" + "a" * 14,
        [
            pltpu.VMEM((2 * slots, width), BF),
            pltpu.VMEM((2 * slots, ff), BF),
            pltpu.VMEM((2 * slots, width), BF),
            pltpu.VMEM((2 * slots, ff), BF),
            pltpu.SemaphoreType.DMA((8,)),
        ],
    )

    def halves(v):
        h = v.shape[1] // 2
        return v[:, :h], v[:, h:]

    def rows_side(a, attn):
        both = jnp.concatenate([a, attn], axis=1)
        pair_rows = jnp.stack([both, across(both)])
        quarter = pair_rows.reshape(2, rows, 2, pair, half)
        own = jnp.where(dpi == 0, quarter[:, :, :, 0], quarter[:, :, :, 1])
        other = jnp.where(dpi == 0, quarter[:, :, :, 1], quarter[:, :, :, 0])
        return jnp.stack([own, along(other)]).reshape(4 * rows, 2, half)

    def cols_side(dq, dr):
        (q_lo, q_hi), (r_lo, r_hi) = halves(dq), halves(dr)
        lo = jnp.concatenate([q_lo, r_lo], axis=1)
        hi = jnp.concatenate([q_hi, r_hi], axis=1)
        two = jnp.stack([jnp.where(is0, lo, hi), across(jnp.where(is0, hi, lo))])
        return jnp.stack([two, along(two)]).reshape(4 * rows, 2 * width)

    def partial_tile(a, attn, dq, dr):
        left, right = rows_side(a, attn), cols_side(dq, dr)
        split = 3 * width // 2
        return jnp.concatenate(
            [dot(left[:, 0].T, right[:, :split]), dot(left[:, 1].T, right[:, split:])], axis=1
        ).astype(BF)

    def shift(v, k):
        return lax.ppermute(v, "expert", [(i, (i + k) % group) for i in range(group)])

    me = lax.axis_index("expert")

    def reduce_all(tile):
        part = tile.shape[0] // group
        blocks = tile.reshape(group, part, tile.shape[1])
        total = lax.dynamic_index_in_dim(blocks, me, 0, keepdims=False).astype(F32)
        for k in range(1, group):
            block = lax.dynamic_index_in_dim(blocks, (me + k) % group, 0, keepdims=False)
            total = total + shift(block, k).astype(F32)
        total = total.astype(BF)
        full = jnp.zeros_like(blocks)
        full = lax.dynamic_update_index_in_dim(full, total, me, 0)
        for k in range(1, group):
            full = lax.dynamic_update_index_in_dim(full, shift(total, k), (me - k) % group, 0)
        return full.reshape(tile.shape)

    tile1 = reduce_all(partial_tile(a1, attn1, dq1, dr1))
    sm_mine = jnp.where(is0, sm0, sm1) + across(jnp.where(is0, sm1, sm0))
    sm_lo, sm_hi = halves(sm_mine)
    sm_half = jnp.where(dpi == 0, sm_lo, sm_hi) + along(jnp.where(dpi == 0, sm_hi, sm_lo))
    sm_cols = jnp.pad(sm_half.T, ((0, 0), (0, -(experts + 2) % 128))).astype(BF)
    tile0 = reduce_all(jnp.concatenate([partial_tile(a0, attn0, dq0, dr0), sm_cols], axis=1))
    small_sum = tile0[:, 2 * width :].astype(F32)
    tile0 = tile0[:, : 2 * width]
    far1, far0 = to_section(tile1, 1), to_section(tile0, 0)
    left_tile = jnp.where(is0, tile0, far1).astype(F32)
    right_tile = jnp.where(is0, far0, tile1).astype(F32)
    split = 3 * width // 2
    grad_qkv = jnp.concatenate([left_tile[:, :split], right_tile[:, :split]], axis=1)
    grad_proj = jnp.concatenate([left_tile[:, split:], right_tile[:, split:]], axis=1)

    mine_end = jnp.where(is0, dh0, out1)[:count]
    other_end = across(jnp.where(is0, out1, dh0)[:count])
    ends = jnp.stack([jnp.where(is0, mine_end, other_end), jnp.where(is0, other_end, mine_end)])
    boundary = ends.reshape(1, micro, images, seq, width)
    return (
        boundary,
        small_sum[:, 0][None],
        grad_qkv[None],
        grad_proj[None],
        small_sum[:, 1][None],
        small_sum[:, 2 : 2 + experts][None],
        gin[None, None],
        gout[None, None],
    )


def solution(mesh):
    in_specs = (
        P(None, ("expert", "dp"), None, None),
        P(None, ("expert", "dp"), None, None),
        P("section", None, ("expert", "dp"), None, None),
        P("section", "dp"),
        P("section", "dp", None),
        P("section", "dp", None),
        P("section", "dp"),
        P("section", "dp", None),
        P("section", "expert", None, "dp"),
        P("section", "expert", "dp", None),
    )
    out_specs = (
        P("section", None, ("expert", "dp"), None, None),
        P("section", "dp"),
        P("section", "dp", None),
        P("section", "dp", None),
        P("section", "dp"),
        P("section", "dp", None),
        P("section", "expert", None, "dp"),
        P("section", "expert", "dp", None),
    )
    return jax.shard_map(shards, mesh=mesh, in_specs=in_specs, out_specs=out_specs, check_vma=False)
```
